32 devices in a mesh: groups: 2 (over x), ctx: 16 (over z, y, core).
Axes of the slice: x: 2, y: 2, z: 4, core: 2. Of those that a mesh axis runs over, the one named last changes fastest.
Arguments:
- query: bfloat16 [4096, 32, 128], P(('groups', 'ctx')), parts along dimension 0, may hold values from -96 to 96
- keys: bfloat16 [4096, 4, 128], P(('groups', 'ctx')), parts along dimension 0, may hold values from -8 to 8
- values: bfloat16 [4096, 4, 128], P(('groups', 'ctx')), parts along dimension 0, may hold values from -6 to 6
- segment: int32 [4096], P(('groups', 'ctx')), parts along dimension 0, may hold values from 0 to 3, never falling along the last dimension, each value on 1 to 768 neighbouring positions
- instr_offset: int32 [8], P('groups'), parts along dimension 0, may hold values from 0 to 65535
- instr_width: int32 [8], P('groups'), parts along dimension 0, may hold values from 1 to 256
- steer: int32 [32], replicated, may hold values 0 or 1
Outputs:
- attended: bfloat16 [4096, 32, 128], P(('groups', 'ctx')), parts along dimension 0
The draws below stay inside these ranges and needn't reach their ends.
There are 2 independent parts, one for each index of `groups`. The reference program is written for one: setup_inputs(seed, part) draws one part's arguments, and reference() takes and returns one part's arrays. A program takes and returns all parts, laid end to end along the dimension named above; an argument that names none is the same for every part. Nothing has to cross between parts.
Inputs may be any that keep to these rules, and one draw needn't show every extreme that they name: `segment`: segment numbers never fall; each of the 4 prompts holds 1 to 768 tokens, and one holds exactly 768.
All inputs are finite; a program needn't handle non-finite values.
Results may differ from the reference program's by a relative error of at most 0.0036.
Values may be sent and summed in bfloat16 or wider, within the bound.
A program may use at most 64 MiB of HBM per device.

```python
import math
import jax
import jax.numpy as jnp
import numpy as np
from jax import lax

TOK_DEV = 128
HEADS = 32
KV_HEADS = 4
HD = 128
DOCS = 4
TOKENS = 2048
BACK = 6
DOC_MOST = 768
N_CTX = 16


def draw_query(key, part):
    own_key = jax.random.fold_in(key, 11)
    result = jnp.clip(jax.random.normal(own_key, (TOKENS, HEADS, HD), jnp.float32), -6.0, 6.0)
    return result.astype(jnp.bfloat16)


def draw_keys(key, part):
    own_key = jax.random.fold_in(key, 13)
    result = jnp.clip(jax.random.normal(own_key, (TOKENS, KV_HEADS, HD), jnp.float32), -6.0, 6.0)
    return result.astype(jnp.bfloat16)


def set_ends(entries, key, low, high):
    index_at = [jax.random.randint(jax.random.fold_in(key, axis), (), 0, length) for axis, length in enumerate(entries.shape)]
    longest = entries.shape.index(max(entries.shape))
    beside = index_at[:longest] + [(index_at[longest] + 1) % entries.shape[longest]] + index_at[longest + 1:]
    return entries.at[tuple(index_at)].set(low).at[tuple(beside)].set(high)


def steps_of(key, dims, shards, low, high):
    gain, own = 1.0, jax.random.fold_in(key, 6)
    for axis_at, blocks in shards:
        draws = jnp.exp(jax.random.uniform(jax.random.fold_in(own, axis_at), (blocks,), jnp.float32, low / len(shards), high / len(shards)))
        gain = gain * jnp.repeat(draws, dims[axis_at] // blocks).reshape([-1 if axis == axis_at else 1 for axis in range(len(dims))])
    return gain


def profile(number_of, total, bound, slope):
    weights = [(1 << 20) // math.isqrt(rank ** slope) + 1 for rank in range(2, number_of + 1)]
    surplus, given = total - bound - (number_of - 1), [1] * (number_of - 1)
    while surplus > 0:
        movable = [i for i in range(number_of - 1) if given[i] < bound]
        mass, budget = sum([weights[i] for i in movable]), surplus
        for i in movable:
            more = min(bound - given[i], max(1, budget * weights[i] // mass), surplus)
            given[i] = given[i] + more
            surplus = surplus - more
    return np.array([bound] + given)


def ragged(rng, count, total, limit, skew):
    if count == 2:
        one = jax.random.randint(rng, (), max(1, total - limit), min(limit, total - 1) + 1)
        return jnp.stack([one, total - one])
    lengths = jnp.asarray(profile(count, total, limit, skew), jnp.int32)
    couples = (count - 1) // 2
    source_of, sink = lengths[1:1 + 2 * couples:2], lengths[2:2 + 2 * couples:2]
    slack = jnp.minimum(source_of - 1, limit - sink)
    passed = jax.random.randint(jax.random.fold_in(rng, 1), (couples,), 0, 1 << 20) % (slack + 1)
    lengths = lengths.at[1:1 + 2 * couples:2].set(source_of - passed).at[2:2 + 2 * couples:2].set(sink + passed)
    return lengths[jax.random.permutation(jax.random.fold_in(rng, 2), count)]


def bell_draw(key, extent, width, bound, split=(), held_as=jnp.bfloat16):
    values = width * jax.random.normal(key, extent, jnp.float32)
    if split:
        values = values * steps_of(key, extent, split, -0.22, 0.18)
    return jnp.clip(values, -bound, bound).astype(held_as)


def setup_inputs(seed: int = 0, part: int = 0) -> dict:
    key_of = jax.random.split(jax.random.key(seed), 8)
    part_splits = jax.random.split(jax.random.fold_in(key_of[7], part), 8)
    return {
        "query": draw_query(jax.random.fold_in(jax.random.fold_in(key_of[7], part), 71), part),
        "keys": draw_keys(jax.random.fold_in(jax.random.fold_in(key_of[7], part), 71), part),
        "values": bell_draw(part_splits[2], (TOKENS, KV_HEADS, HD), 1.0, 6.0, ((0, 16),)),
        "segment": jnp.searchsorted(jnp.cumsum(ragged(part_splits[3], DOCS, TOKENS, DOC_MOST, 2)), jnp.arange(TOKENS), side="right").astype(jnp.int32),
        "instr_offset": set_ends(jax.random.randint(part_splits[4], (DOCS,), 0, 65536), jax.random.fold_in(part_splits[4], 1), 0, 65535).astype(jnp.int32),
        "instr_width": set_ends(jax.random.randint(part_splits[5], (DOCS,), 1, 2 * TOK_DEV + 1), jax.random.fold_in(part_splits[5], 1), 1, 2 * TOK_DEV).astype(jnp.int32),
        "steer": set_ends((jax.random.randint(key_of[6], (HEADS,), 0, 2) < 1).astype(jnp.int32), jax.random.fold_in(key_of[6], 1), 0, 1),
    }


NEG_BIG = -1.0e30
LOG_COEF = -4.605170185988091


def reference(query, keys, values, segment, instr_offset, instr_width, steer):
    head_count = query.shape[1]
    head_width = query.shape[2]
    kv_count = keys.shape[1]
    ratio = head_count // kv_count
    labels = jnp.arange(DOCS, dtype=jnp.int32)
    counts = jnp.sum((segment[:, None] == labels[None, :]).astype(jnp.int32), axis=0)
    starts = jnp.cumsum(counts) - counts
    instr_lo = starts + instr_offset % counts
    instr_hi = jnp.minimum(instr_lo + instr_width, starts + counts)
    margin = BACK * TOK_DEV
    keys_pad = jnp.concatenate([jnp.zeros((margin, kv_count, head_width), keys.dtype), keys], axis=0)
    values_pad = jnp.concatenate([jnp.zeros((margin, kv_count, head_width), values.dtype), values], axis=0)
    seg_pad = jnp.concatenate([jnp.full((margin,), -1, jnp.int32), segment.astype(jnp.int32)], axis=0)
    steer_gain = steer.astype(jnp.float32).reshape(kv_count, ratio)

    def one_block(block):
        start = (block * TOK_DEV).astype(jnp.int32)
        query_grouped_rows = lax.dynamic_slice_in_dim(query, start, TOK_DEV, 0).astype(jnp.float32)
        query_grouped_rows = query_grouped_rows.reshape(TOK_DEV, kv_count, ratio, head_width)
        key_block_rows = lax.dynamic_slice_in_dim(keys_pad, start, margin + TOK_DEV, 0).astype(jnp.float32)
        value_block_rows = lax.dynamic_slice_in_dim(values_pad, start, margin + TOK_DEV, 0).astype(jnp.float32)
        key_seg = lax.dynamic_slice_in_dim(seg_pad, start, margin + TOK_DEV, 0)
        query_seg = lax.dynamic_slice_in_dim(segment.astype(jnp.int32), start, TOK_DEV, 0)
        query_pos = start + jnp.arange(TOK_DEV, dtype=jnp.int32)
        key_pos = start - margin + jnp.arange(margin + TOK_DEV, dtype=jnp.int32)
        picked = key_seg[:, None] == labels[None, :]
        low_edge = jnp.sum(jnp.where(picked, instr_lo[None, :], 0), axis=1)
        high_edge = jnp.sum(jnp.where(picked, instr_hi[None, :], 0), axis=1)
        inside = (key_pos >= low_edge) & (key_pos < high_edge)
        allowed = (key_seg[None, :] == query_seg[:, None]) & (key_pos[None, :] <= query_pos[:, None])
        logit_scores = jnp.einsum("aecy,uey->ecau", query_grouped_rows, key_block_rows, precision=lax.Precision.HIGHEST)
        logit_scores = logit_scores * (head_width ** -0.5)
        bias = steer_gain[:, :, None, None] * jnp.where(inside, 0.0, LOG_COEF)[None, None, None, :]
        logit_scores = jnp.where(allowed[None, None], logit_scores + bias, NEG_BIG)
        top = jnp.max(logit_scores, axis=3, keepdims=True)
        probs = jnp.where(allowed[None, None], jnp.exp(logit_scores - top), 0.0)
        denom = jnp.sum(probs, axis=3, keepdims=True)
        probs_lowered_precision = lax.optimization_barrier(probs.astype(jnp.bfloat16)).astype(jnp.float32)
        output_running_sum = jnp.einsum("cfqj,jcz->cfqz", probs_lowered_precision, value_block_rows, precision=lax.Precision.HIGHEST)
        result = (output_running_sum / denom).astype(jnp.bfloat16)
        return result.transpose(2, 0, 1, 3).reshape(TOK_DEV, head_count, head_width)

    blocks = lax.map(one_block, jnp.arange(N_CTX, dtype=jnp.int32))
    return blocks.reshape(query.shape[0], head_count, head_width)
```

```python
import jax
import jax.numpy as jnp
import numpy as np
from jax import lax
from jax.experimental import pallas as pl
from jax.experimental.pallas import tpu as pltpu
from jax.sharding import PartitionSpec as P

NEG_BIG = -1e30
LOG_COEF = -4.605170185988091
LOG2E = 1.4426950408889634
TILES = 4


def passed_along(value, axis, steps):
    count = lax.axis_size(axis)
    initial, last = (max(0, -steps), min(count, count - steps))
    return lax.ppermute(value, axis, [(source, source + steps) for source in range(initial, last)])


def prompt_tables(segment, instr_offset, instr_width):
    labels = jnp.arange(instr_offset.shape[0], dtype=jnp.int32)
    local_counts = jnp.sum((segment[:, None] == labels[None, :]).astype(jnp.int32), axis=0)
    counts = lax.psum(local_counts, "ctx")
    starts = jnp.cumsum(counts) - counts
    instr_lo = starts + instr_offset % counts
    instr_hi = jnp.minimum(instr_lo + instr_width, starts + counts)
    return (starts, instr_lo, instr_hi, labels)


def key_flags(key_pos, tables):
    starts, instr_lo, instr_hi, labels = tables
    key_seg = jnp.sum((starts[None, :] <= key_pos[:, None]).astype(jnp.int32), axis=1) - 1
    picked = key_seg[:, None] == labels[None, :]
    low_edge = jnp.sum(jnp.where(picked, instr_lo[None, :], 0), axis=1)
    high_edge = jnp.sum(jnp.where(picked, instr_hi[None, :], 0), axis=1)
    return (key_seg, (key_pos >= low_edge) & (key_pos < high_edge))


def update(carry_state, query_grouped_rows, key_value_block_length, allowed, inside, steer_gain):
    running, total, output_running_sum = carry_state
    logit_scores = jnp.einsum(
        "aecy,uey->ecau",
        query_grouped_rows,
        key_value_block_length[0],
        preferred_element_type=jnp.float32,
    )
    logit_scores = logit_scores * query_grouped_rows.shape[3] ** (-0.5)
    bias = steer_gain[:, :, None, None] * jnp.where(inside, 0.0, LOG_COEF)[None, None, None, :]
    logit_scores = jnp.where(allowed[None, None], logit_scores + bias, NEG_BIG)
    new_max = jnp.maximum(running, jnp.max(logit_scores, axis=3, keepdims=True))
    shrink = jnp.exp(running - new_max)
    probs = jnp.where(allowed[None, None], jnp.exp(logit_scores - new_max), 0.0)
    total = total * shrink + jnp.sum(probs, axis=3, keepdims=True)
    weighted = jnp.einsum(
        "cfqj,jcz->cfqz",
        probs.astype(jnp.bfloat16),
        key_value_block_length[1],
        preferred_element_type=jnp.float32,
    )
    return (new_max, total, output_running_sum * shrink + weighted)


def ring_device(query, keys, values, segment, instr_offset, instr_width, steer):
    tok_rows = query.shape[0]
    head_count = query.shape[1]
    head_width = query.shape[2]
    kv_count = keys.shape[1]
    ratio = head_count // kv_count
    reach_most = 3 * lax.axis_size("ctx") // 8
    query_grouped_rows = query.reshape(tok_rows, kv_count, ratio, head_width)
    position = lax.axis_index("ctx")
    offsets = jnp.arange(tok_rows, dtype=jnp.int32)
    query_pos = position * tok_rows + offsets
    tables = prompt_tables(segment, instr_offset, instr_width)
    steer_gain = steer.astype(jnp.float32).reshape(kv_count, ratio)
    stat_shape = (kv_count, ratio, tok_rows, 1)
    carry_state = (
        jnp.full(stat_shape, NEG_BIG, jnp.float32),
        jnp.zeros(stat_shape, jnp.float32),
        jnp.zeros((kv_count, ratio, tok_rows, head_width), jnp.float32),
    )

    def visit(held_state, key_value_block_length, hops_back):
        key_pos = (position - hops_back) * tok_rows + offsets
        key_seg, inside = key_flags(key_pos, tables)
        allowed = (key_seg[None, :] == segment[:, None]) & (key_pos[None, :] <= query_pos[:, None])
        return update(
            held_state, query_grouped_rows, key_value_block_length, allowed, inside, steer_gain
        )

    own_kv = jnp.stack([keys, values])
    carry_state = visit(carry_state, own_kv, 0)

    def loop_step(hop_count, loop_carry):
        held_state, current_kv = loop_carry
        current_kv = passed_along(current_kv, "ctx", 1)
        return (visit(held_state, current_kv, hop_count), current_kv)

    carry_state, _ = lax.fori_loop(1, reach_most + 1, loop_step, (carry_state, own_kv))
    running, total, output_running_sum = carry_state
    result = (output_running_sum / total).astype(jnp.bfloat16)
    return result.transpose(2, 0, 1, 3).reshape(tok_rows, head_count, head_width)


def bias_parts(width):
    left, parts = LOG_COEF * width ** 0.5, []
    for _ in range(3):
        parts.append(float(np.float32(left).astype(jnp.bfloat16)))
        left = left - parts[-1]
    return parts


def block_kernel(
    q_hbm, k_hbm, v_hbm, seg_hbm, steer_hbm, off_hbm, width_hbm,
    out_ref,
    q_raw, q_s, kv_raw, kv_wide, own, near, mid, rest, seg_all, pen, k_more, m_s, acc,
    steer_ref, off_ref, width_ref,
    in_sem, seg_send, seg_recv, link_recv, pair_recv, own_send, fwd_send, known,
):
    count = lax.axis_size("ctx")
    kv_count, tok = own.shape[0], own.shape[2]
    width = own.shape[3]
    ratio = q_raw.shape[1] // kv_count
    docs = off_ref.shape[0]
    parts = bias_parts(width)
    me = lax.axis_index("ctx")
    core = lax.rem(me, 2)
    chip = me // 2
    col = lax.rem(chip, 2)
    plane = chip // 2
    partner = me + 1 - 2 * core
    across = me + 2 - 4 * col
    ahead = me + 4
    behind = me - 4
    planes = count // 4
    chips = count // 2
    pair0 = 2 * chip

    def remote(src, dst, send, recv, target):
        return pltpu.make_async_remote_copy(
            src_ref=src, dst_ref=dst, send_sem=send, recv_sem=recv,
            device_id={"ctx": target}, device_id_type=pl.DeviceIdType.MESH,
        )

    has_ahead = ahead < count
    has_mid = plane >= 1
    has_near = chip >= 1
    has_rest = chip >= 3
    beside = jnp.minimum(plane, 1) + jnp.minimum(planes - 1 - plane, 1)

    def tell(sem, target):
        pl.semaphore_signal(
            sem, inc=1, device_id={"ctx": target}, device_id_type=pl.DeviceIdType.MESH
        )

    def tell_lane(sem):
        tell(sem, across)

        @pl.when(has_ahead)
        def _():
            tell(sem, ahead)

        @pl.when(has_mid)
        def _():
            tell(sem, behind)

    local_k = pltpu.make_async_copy(k_hbm, kv_raw.at[0], in_sem.at[1])
    local_v = pltpu.make_async_copy(v_hbm, kv_raw.at[1], in_sem.at[3])
    local_seg = pltpu.make_async_copy(seg_hbm, seg_all.at[me], in_sem.at[2])
    local_q = pltpu.make_async_copy(q_hbm, q_raw, in_sem.at[0])
    smalls = [
        pltpu.make_async_copy(src, dst, in_sem.at[4 + n])
        for n, (src, dst) in enumerate(
            ((steer_hbm, steer_ref), (off_hbm, off_ref), (width_hbm, width_ref))
        )
    ]
    local_k.start()
    local_v.start()
    seg_all[...] = jnp.full(seg_all.shape, -1, jnp.int32)
    barrier = pltpu.get_barrier_semaphore()
    tell(barrier, partner)
    tell_lane(barrier)
    local_seg.start()
    local_q.start()
    for small in smalls:
        small.start()

    @pl.when(jnp.logical_not(has_mid))
    def _():
        mid[...] = jnp.zeros_like(mid)

    @pl.when(jnp.logical_not(has_near))
    def _():
        near[...] = jnp.zeros_like(near)

    @pl.when(jnp.logical_not(has_rest))
    def _():
        rest[1] = jnp.zeros_like(rest[1])

    @pl.when(jnp.logical_not(has_rest) & (core == 0))
    def _():
        rest[0] = jnp.zeros_like(rest[0])

    for n, local in enumerate((local_k, local_v)):
        local.wait()
        kv_wide[n] = kv_raw[n].astype(jnp.float32)
        for h in range(kv_count):
            rows = kv_wide[n, pl.ds(h, tok, stride=kv_count), :]
            own[h, n] = rows.astype(jnp.bfloat16)

    pl.semaphore_wait(barrier, 2 + beside)

    def own_ahead(h):
        return remote(own.at[h], mid.at[core, h], own_send.at[0, h], link_recv.at[0, h], ahead)

    def own_across(h):
        return remote(own.at[h], near.at[core, h], own_send.at[1, h], link_recv.at[1, h], across)

    def own_pair(h):
        return remote(own.at[h], rest.at[0, h], own_send.at[2, h], pair_recv.at[2, h], partner)

    def mid_pair(h):
        return remote(mid.at[core, h], mid.at[core, h], fwd_send.at[0, h], pair_recv.at[0, h], partner)

    def mid_across(h):
        return remote(mid.at[core, h], near.at[core, h], fwd_send.at[1, h], link_recv.at[1, h], across)

    def near_pair(h):
        return remote(near.at[core, h], near.at[core, h], fwd_send.at[2, h], pair_recv.at[1, h], partner)

    def near_ahead(h):
        return remote(near.at[core, h], rest.at[core, h], fwd_send.at[3, h], link_recv.at[2, h], ahead)

    def rest_pair(h):
        return remote(rest.at[1, h], rest.at[1, h], fwd_send.at[4, h], pair_recv.at[2, h], partner)

    def arrived_link(kind, buf, slot, h):
        remote(buf.at[slot, h], buf.at[slot, h], own_send.at[0, h], link_recv.at[kind, h], partner).wait_recv()

    def arrived_pair(kind, buf, slot, h):
        remote(buf.at[slot, h], buf.at[slot, h], own_send.at[0, h], pair_recv.at[kind, h], partner).wait_recv()

    def seg_pair():
        return remote(seg_all.at[me], seg_all.at[me], seg_send.at[0], seg_recv.at[0], partner)

    def seg_copy(slot, step):
        both = seg_all.at[pl.ds(pair0, 2)]
        return remote(both, both, seg_send.at[slot], seg_recv.at[slot], me + 2 * step)

    def seg_came(slot, step):
        both = seg_all.at[pl.ds(pair0 - 2 * step, 2)]
        remote(both, both, seg_send.at[slot], seg_recv.at[slot], partner).wait_recv()

    steps = [(1, 1), (2, -1), (3, 2), (4, -2), (5, 3), (6, -3)]

    def inside_row(step):
        return (chip + step >= 0) & (chip + step < chips)

    def seg_some(picked):
        for slot, step in picked:
            @pl.when(inside_row(step))
            def _():
                seg_copy(slot, step).start()

    def send_own(h):
        @pl.when(has_ahead)
        def _():
            own_ahead(h).start()

        @pl.when(col == 0)
        def _():
            own_across(h).start()

    tell_lane(known.at[0])
    local_seg.wait()
    seg_pair().start()
    send_own(0)
    remote(
        seg_all.at[partner], seg_all.at[partner], seg_send.at[0], seg_recv.at[0], partner
    ).wait_recv()
    pl.semaphore_wait(known.at[0], 1 + beside)
    tell_lane(known.at[1])
    seg_some(steps[2:4])
    seg_some(steps[:2])
    send_own(1)
    pl.semaphore_wait(known.at[1], 1 + beside)
    seg_some(steps[4:])
    for h in range(2, kv_count):
        send_own(h)

    @pl.when(core == 0)
    def _():
        for h in range(kv_count):
            own_pair(h).start()

    for small in smalls:
        small.wait()
    lane = lax.broadcasted_iota(jnp.int32, (tok, tok), 1)
    mine = jnp.broadcast_to(seg_all[me], (tok, tok)).astype(jnp.float32)
    mine = jnp.transpose(mine)
    belongs = jnp.where(mine == lane.astype(jnp.float32), 1.0, 0.0)
    lane8 = lax.broadcasted_iota(jnp.int32, (ratio, tok), 1)
    row8 = lax.broadcasted_iota(jnp.int32, (ratio, tok), 0)
    local_q.wait()
    for h in range(kv_count):
        q_s[h, :, :width] = q_raw[:, ratio * h:ratio * (h + 1), :].reshape(tok * ratio, width)
        gain = jnp.zeros((ratio, tok), jnp.float32)
        for r in range(ratio):
            gain = jnp.where(row8 == r, steer_ref[ratio * h + r].astype(jnp.float32), gain)
        gain = jnp.where((lane8 >= docs) & (lane8 < docs + len(parts)), gain, 0.0)
        more = belongs[:, None, :] + gain[None]
        q_s[h, :, width:] = more.reshape(tok * ratio, tok).astype(jnp.bfloat16)

    def take_mid(h):
        @pl.when(has_mid)
        def _():
            arrived_link(0, mid, core, h)

            @pl.when(col == 1)
            def _():
                mid_across(h).start()
            mid_pair(h).start()

    def take_near(h):
        @pl.when(has_near)
        def _():
            arrived_link(1, near, core, h)

            @pl.when(has_ahead)
            def _():
                near_ahead(h).start()
            near_pair(h).start()

    def take_rest(h):
        @pl.when(has_rest & (core == 1))
        def _():
            arrived_link(2, rest, core, h)
            rest_pair(h).start()

    take_mid(0)
    take_mid(1)
    for slot, step in steps:
        @pl.when(inside_row(-step))
        def _():
            seg_came(slot, step)

    every = seg_all[:, 0, :]
    low, high = [], []
    row_low = jnp.zeros((ratio, tok), jnp.int32)
    row_high = jnp.zeros((ratio, tok), jnp.int32)
    before = 2 * tok * jnp.maximum(chip - 3, 0)
    for s in range(docs):
        many = jnp.sum((every == s).astype(jnp.int32))
        low.append(before + lax.rem(off_ref[s], jnp.maximum(many, 1)))
        row_low = jnp.where(row8 == s, before, row_low)
        before = before + many
        row_high = jnp.where(row8 == s, before, row_high)
        high.append(jnp.minimum(low[s] + width_ref[s], before))
    row_part = jnp.zeros((ratio, tok), jnp.float32)
    for n, part in enumerate(parts):
        row_part = jnp.where(row8 == docs + n, part, row_part)
    blocks = (
        me, pair0 - 4, pair0 - 3, pair0 - 2, pair0 - 1,
        jnp.where(core == 0, pair0 - 6, pair0), pair0 - 5,
    )
    padding = jnp.zeros((tok - ratio, tok), jnp.float32)
    for slot, block in enumerate(blocks):
        key_pos = block * tok + lane8
        inside = (key_pos >= low[0]) & (key_pos < high[0])
        for s in range(1, docs):
            inside = inside | ((key_pos >= low[s]) & (key_pos < high[s]))
        outside = (key_pos < row_low) | (key_pos >= row_high)
        seg_rows = jnp.where(outside, NEG_BIG, 0.0)
        part_rows = jnp.where(inside, 0.0, row_part)
        rows = jnp.where(row8 < docs, seg_rows, part_rows)
        rows = jnp.transpose(jnp.concatenate([rows, padding], axis=0))
        k_more[slot * tok:(slot + 1) * tok, :] = rows.astype(jnp.bfloat16)
    later = lane > lax.broadcasted_iota(jnp.int32, (tok, tok), 0)
    pen[...] = jnp.where(later, NEG_BIG, 0.0)

    factor = width ** (-0.5) * LOG2E
    tok_t = tok // TILES
    row_t = tok_t * ratio

    def visit(h, refs, slot, first):
        size = len(refs) * tok

        key = jnp.concatenate([ref[0] for ref in refs], axis=0)
        key = jnp.concatenate([key, k_more[slot * tok:slot * tok + size, :]], axis=1)
        value = jnp.concatenate([ref[1] for ref in refs], axis=0)
        value = jnp.concatenate([value, jnp.ones_like(value)], axis=1)

        def scores(i):
            return lax.dot_general(
                q_s[h, i * row_t:(i + 1) * row_t, :], key, (((1,), (1,)), ((), ())),
                preferred_element_type=jnp.float32,
            ).reshape(tok_t, ratio, size)

        following = scores(0)
        for i in range(TILES):
            toks = slice(i * tok_t, (i + 1) * tok_t)
            raw = following
            if i + 1 < TILES:
                following = scores(i + 1)
            pieces = [raw[:, :, n * tok:(n + 1) * tok] for n in range(len(refs))]
            if first:
                pieces[0] = pieces[0] + pen[toks, :][:, None, :]
            peak = pieces[0]
            for piece in pieces[1:]:
                peak = jnp.maximum(peak, piece)
            peak = jnp.max(peak, axis=2, keepdims=True)
            if first:
                top = jnp.broadcast_to(peak, (tok_t, ratio, tok))
                m_s[h, toks] = top
            else:
                held = m_s[h, toks]
                top = jnp.maximum(held, peak)
                shrink = jnp.exp2((held - top) * factor)
            packed = jnp.concatenate(
                [
                    jnp.exp2((piece - top) * factor).reshape(row_t, tok).astype(jnp.bfloat16)
                    for piece in pieces
                ],
                axis=1,
            )
            both = jnp.dot(packed, value, preferred_element_type=jnp.float32)
            both = both.reshape(tok_t, ratio, 2 * width)
            if first:
                acc[h, toks] = both
            else:
                weighted = both[:, :, :width] + acc[h, toks, :, :width] * shrink
                total = both[:, :, width:] + acc[h, toks, :, width:] * shrink
                heads = slice(ratio * h, ratio * (h + 1))
                out_ref[toks, heads, :] = (weighted / total).astype(jnp.bfloat16)

    def visit_early(h):
        @pl.when(has_mid)
        def _():
            arrived_pair(0, mid, 1 - core, h)
        visit(h, [own.at[h], mid.at[0, h], mid.at[1, h]], 0, True)

    def visit_late(h):
        @pl.when(has_near)
        def _():
            arrived_pair(1, near, 1 - core, h)

        @pl.when(has_rest & (core == 0))
        def _():
            arrived_link(2, rest, core, h)

        @pl.when((core == 1) | has_rest)
        def _():
            arrived_pair(2, rest, 1 - core, h)
        visit(h, [near.at[0, h], near.at[1, h], rest.at[0, h], rest.at[1, h]], 3, False)

    last = kv_count - 1
    take_mid(2)
    for h in range(kv_count):
        if h == last:
            take_rest(0)
        visit_early(h)
        if h == 0:
            take_near(0)
            take_mid(last)
        if h < last:
            take_near(h + 1)
    for h in range(kv_count):
        if h < last:
            take_rest(h + 1)
        visit_late(h)

    seg_pair().wait_send()
    for slot, step in steps:
        @pl.when(inside_row(step))
        def _():
            seg_copy(slot, step).wait_send()

    for h in range(kv_count):
        @pl.when(has_ahead)
        def _():
            own_ahead(h).wait_send()

        @pl.when(col == 0)
        def _():
            own_across(h).wait_send()

        @pl.when(core == 0)
        def _():
            own_pair(h).wait_send()

        @pl.when(has_mid)
        def _():
            mid_pair(h).wait_send()

        @pl.when(has_mid & (col == 1))
        def _():
            mid_across(h).wait_send()

        @pl.when(has_near)
        def _():
            near_pair(h).wait_send()

        @pl.when(has_near & has_ahead)
        def _():
            near_ahead(h).wait_send()

        @pl.when(has_rest & (core == 1))
        def _():
            rest_pair(h).wait_send()


def plane_device(query, keys, values, segment, instr_offset, instr_width, steer):
    tok, heads, width = query.shape
    kv_count = keys.shape[1]
    ratio = heads // kv_count
    count = lax.axis_size("ctx")
    keys, values = keys.reshape(tok * kv_count, width), values.reshape(tok * kv_count, width)
    hbm = pl.BlockSpec(memory_space=pltpu.HBM)
    pair = pltpu.VMEM((2, kv_count, 2, tok, width), jnp.bfloat16)
    dma = pltpu.SemaphoreType.DMA
    return pl.pallas_call(
        block_kernel,
        out_shape=jax.ShapeDtypeStruct(query.shape, query.dtype),
        in_specs=[hbm] * 7,
        out_specs=pl.BlockSpec(memory_space=pltpu.VMEM),
        scratch_shapes=[
            pltpu.VMEM(query.shape, jnp.bfloat16),
            pltpu.VMEM((kv_count, tok * ratio, 2 * width), jnp.bfloat16),
            pltpu.VMEM((2, tok * kv_count, width), jnp.bfloat16),
            pltpu.VMEM((2, tok * kv_count, width), jnp.float32),
            pltpu.VMEM((kv_count, 2, tok, width), jnp.bfloat16),
            pair, pair, pair,
            pltpu.VMEM((count, 1, tok), jnp.int32),
            pltpu.VMEM((tok, tok), jnp.float32),
            pltpu.VMEM((7 * tok, tok), jnp.bfloat16),
            pltpu.VMEM((kv_count, tok, ratio, width), jnp.float32),
            pltpu.VMEM((kv_count, tok, ratio, 2 * width), jnp.float32),
            pltpu.SMEM(steer.shape, jnp.int32),
            pltpu.SMEM(instr_offset.shape, jnp.int32),
            pltpu.SMEM(instr_width.shape, jnp.int32),
            dma((7,)), dma((7,)), dma((7,)),
            dma((3, kv_count)), dma((3, kv_count)), dma((3, kv_count)), dma((5, kv_count)),
            pltpu.SemaphoreType.REGULAR((2,)),
        ],
        compiler_params=pltpu.CompilerParams(
            collective_id=0, has_side_effects=True, vmem_limit_bytes=55000000
        ),
    )(*[pltpu.with_memory_space_constraint(x, pltpu.HBM) for x in (query, keys, values, segment.reshape(1, tok), steer, instr_offset, instr_width)])


def per_device(query, keys, values, segment, instr_offset, instr_width, steer):
    plan = plane_device if lax.axis_size("ctx") == 16 else ring_device
    return plan(query, keys, values, segment, instr_offset, instr_width, steer)


def solution(mesh):
    in_specs = (
        P(("groups", "ctx"), None, None),
        P(("groups", "ctx"), None, None),
        P(("groups", "ctx"), None, None),
        P(("groups", "ctx")),
        P("groups"),
        P("groups"),
        P(),
    )
    out_specs = P(("groups", "ctx"), None, None)
    return jax.shard_map(
        per_device, mesh=mesh, in_specs=in_specs, out_specs=out_specs, check_vma=False
    )
```

```python
import jax
import jax.numpy as jnp
import numpy as np
from jax import lax
from jax.experimental import pallas as pl
from jax.experimental.pallas import tpu as pltpu
from jax.sharding import PartitionSpec as P

NEG_BIG = -1e30
LOG_COEF = -4.605170185988091
LOG2E = 1.4426950408889634
TILES = 4


def passed_along(value, axis, steps):
    count = lax.axis_size(axis)
    initial, last = (max(0, -steps), min(count, count - steps))
    return lax.ppermute(value, axis, [(source, source + steps) for source in range(initial, last)])


def prompt_tables(segment, instr_offset, instr_width):
    labels = jnp.arange(instr_offset.shape[0], dtype=jnp.int32)
    local_counts = jnp.sum((segment[:, None] == labels[None, :]).astype(jnp.int32), axis=0)
    counts = lax.psum(local_counts, "ctx")
    starts = jnp.cumsum(counts) - counts
    instr_lo = starts + instr_offset % counts
    instr_hi = jnp.minimum(instr_lo + instr_width, starts + counts)
    return (starts, instr_lo, instr_hi, labels)


def key_flags(key_pos, tables):
    starts, instr_lo, instr_hi, labels = tables
    key_seg = jnp.sum((starts[None, :] <= key_pos[:, None]).astype(jnp.int32), axis=1) - 1
    picked = key_seg[:, None] == labels[None, :]
    low_edge = jnp.sum(jnp.where(picked, instr_lo[None, :], 0), axis=1)
    high_edge = jnp.sum(jnp.where(picked, instr_hi[None, :], 0), axis=1)
    return (key_seg, (key_pos >= low_edge) & (key_pos < high_edge))


def update(carry_state, query_grouped_rows, key_value_block_length, allowed, inside, steer_gain):
    running, total, output_running_sum = carry_state
    logit_scores = jnp.einsum(
        "aecy,uey->ecau",
        query_grouped_rows,
        key_value_block_length[0],
        preferred_element_type=jnp.float32,
    )
    logit_scores = logit_scores * query_grouped_rows.shape[3] ** (-0.5)
    bias = steer_gain[:, :, None, None] * jnp.where(inside, 0.0, LOG_COEF)[None, None, None, :]
    logit_scores = jnp.where(allowed[None, None], logit_scores + bias, NEG_BIG)
    new_max = jnp.maximum(running, jnp.max(logit_scores, axis=3, keepdims=True))
    shrink = jnp.exp(running - new_max)
    probs = jnp.where(allowed[None, None], jnp.exp(logit_scores - new_max), 0.0)
    total = total * shrink + jnp.sum(probs, axis=3, keepdims=True)
    weighted = jnp.einsum(
        "cfqj,jcz->cfqz",
        probs.astype(jnp.bfloat16),
        key_value_block_length[1],
        preferred_element_type=jnp.float32,
    )
    return (new_max, total, output_running_sum * shrink + weighted)


def ring_device(query, keys, values, segment, instr_offset, instr_width, steer):
    tok_rows = query.shape[0]
    head_count = query.shape[1]
    head_width = query.shape[2]
    kv_count = keys.shape[1]
    ratio = head_count // kv_count
    reach_most = 3 * lax.axis_size("ctx") // 8
    query_grouped_rows = query.reshape(tok_rows, kv_count, ratio, head_width)
    position = lax.axis_index("ctx")
    offsets = jnp.arange(tok_rows, dtype=jnp.int32)
    query_pos = position * tok_rows + offsets
    tables = prompt_tables(segment, instr_offset, instr_width)
    steer_gain = steer.astype(jnp.float32).reshape(kv_count, ratio)
    stat_shape = (kv_count, ratio, tok_rows, 1)
    carry_state = (
        jnp.full(stat_shape, NEG_BIG, jnp.float32),
        jnp.zeros(stat_shape, jnp.float32),
        jnp.zeros((kv_count, ratio, tok_rows, head_width), jnp.float32),
    )

    def visit(held_state, key_value_block_length, hops_back):
        key_pos = (position - hops_back) * tok_rows + offsets
        key_seg, inside = key_flags(key_pos, tables)
        allowed = (key_seg[None, :] == segment[:, None]) & (key_pos[None, :] <= query_pos[:, None])
        return update(
            held_state, query_grouped_rows, key_value_block_length, allowed, inside, steer_gain
        )

    own_kv = jnp.stack([keys, values])
    carry_state = visit(carry_state, own_kv, 0)

    def loop_step(hop_count, loop_carry):
        held_state, current_kv = loop_carry
        current_kv = passed_along(current_kv, "ctx", 1)
        return (visit(held_state, current_kv, hop_count), current_kv)

    carry_state, _ = lax.fori_loop(1, reach_most + 1, loop_step, (carry_state, own_kv))
    running, total, output_running_sum = carry_state
    result = (output_running_sum / total).astype(jnp.bfloat16)
    return result.transpose(2, 0, 1, 3).reshape(tok_rows, head_count, head_width)


def bias_parts(width):
    left, parts = LOG_COEF * width ** 0.5, []
    for _ in range(3):
        parts.append(float(np.float32(left).astype(jnp.bfloat16)))
        left = left - parts[-1]
    return parts


def block_kernel(
    q_hbm, k_hbm, v_hbm, seg_hbm, steer_hbm, off_hbm, width_hbm,
    out_ref,
    q_raw, q_s, kv_raw, kv_wide, own, near, mid, rest, seg_all, pen, k_more, m_s, acc,
    steer_ref, off_ref, width_ref,
    in_sem, seg_send, seg_recv, link_recv, pair_recv, own_send, fwd_send, known,
):
    count = lax.axis_size("ctx")
    kv_count, tok = own.shape[0], own.shape[2]
    width = own.shape[3]
    ratio = q_raw.shape[1] // kv_count
    docs = off_ref.shape[0]
    parts = bias_parts(width)
    me = lax.axis_index("ctx")
    core = lax.rem(me, 2)
    chip = me // 2
    col = lax.rem(chip, 2)
    plane = chip // 2
    partner = me + 1 - 2 * core
    across = me + 2 - 4 * col
    ahead = me + 4
    behind = me - 4
    planes = count // 4
    chips = count // 2
    pair0 = 2 * chip

    def remote(src, dst, send, recv, target):
        return pltpu.make_async_remote_copy(
            src_ref=src, dst_ref=dst, send_sem=send, recv_sem=recv,
            device_id={"ctx": target}, device_id_type=pl.DeviceIdType.MESH,
        )

    has_ahead = ahead < count
    has_mid = plane >= 1
    has_near = chip >= 1
    has_rest = chip >= 3
    beside = jnp.minimum(plane, 1) + jnp.minimum(planes - 1 - plane, 1)

    def tell(sem, target):
        pl.semaphore_signal(
            sem, inc=1, device_id={"ctx": target}, device_id_type=pl.DeviceIdType.MESH
        )

    def tell_planes(to_ahead, to_behind):
        @pl.when(has_ahead)
        def _():
            tell(to_ahead, ahead)

        @pl.when(has_mid)
        def _():
            tell(to_behind, behind)

    local_k = pltpu.make_async_copy(k_hbm, kv_raw.at[0], in_sem.at[1])
    local_v = pltpu.make_async_copy(v_hbm, kv_raw.at[1], in_sem.at[3])
    local_seg = pltpu.make_async_copy(seg_hbm, seg_all.at[me], in_sem.at[2])
    local_q = pltpu.make_async_copy(q_hbm, q_raw, in_sem.at[0])
    smalls = [
        pltpu.make_async_copy(src, dst, in_sem.at[4 + n])
        for n, (src, dst) in enumerate(
            ((steer_hbm, steer_ref), (off_hbm, off_ref), (width_hbm, width_ref))
        )
    ]
    local_k.start()
    local_v.start()
    seg_all[...] = jnp.full(seg_all.shape, -1, jnp.int32)
    barrier = pltpu.get_barrier_semaphore()
    tell(barrier, partner)
    tell(barrier, across)
    tell_planes(barrier, barrier)
    local_seg.start()
    local_q.start()
    for small in smalls:
        small.start()

    @pl.when(jnp.logical_not(has_mid))
    def _():
        mid[...] = jnp.zeros_like(mid)

    @pl.when(jnp.logical_not(has_near))
    def _():
        near[...] = jnp.zeros_like(near)

    @pl.when(jnp.logical_not(has_rest))
    def _():
        rest[1] = jnp.zeros_like(rest[1])

    @pl.when(jnp.logical_not(has_rest) & (core == 0))
    def _():
        rest[0] = jnp.zeros_like(rest[0])

    for n, local in enumerate((local_k, local_v)):
        local.wait()
        kv_wide[n] = kv_raw[n].astype(jnp.float32)
        for h in range(kv_count):
            rows = kv_wide[n, pl.ds(h, tok, stride=kv_count), :]
            own[h, n] = rows.astype(jnp.bfloat16)

    pl.semaphore_wait(barrier, 2 + beside)

    def own_ahead(h):
        return remote(own.at[h], mid.at[core, h], own_send.at[0, h], link_recv.at[0, h], ahead)

    def own_across(h):
        return remote(own.at[h], near.at[core, h], own_send.at[1, h], link_recv.at[1, h], across)

    def own_pair(h):
        return remote(own.at[h], rest.at[0, h], own_send.at[2, h], pair_recv.at[2, h], partner)

    def mid_pair(h):
        return remote(mid.at[core, h], mid.at[core, h], fwd_send.at[0, h], pair_recv.at[0, h], partner)

    def mid_across(h):
        return remote(mid.at[core, h], near.at[core, h], fwd_send.at[1, h], link_recv.at[1, h], across)

    def near_pair(h):
        return remote(near.at[core, h], near.at[core, h], fwd_send.at[2, h], pair_recv.at[1, h], partner)

    def near_ahead(h):
        return remote(near.at[core, h], rest.at[core, h], fwd_send.at[3, h], link_recv.at[2, h], ahead)

    def rest_pair(h):
        return remote(rest.at[1, h], rest.at[1, h], fwd_send.at[4, h], pair_recv.at[2, h], partner)

    def arrived_link(kind, buf, slot, h):
        remote(buf.at[slot, h], buf.at[slot, h], own_send.at[0, h], link_recv.at[kind, h], partner).wait_recv()

    def arrived_pair(kind, buf, slot, h):
        remote(buf.at[slot, h], buf.at[slot, h], own_send.at[0, h], pair_recv.at[kind, h], partner).wait_recv()

    def seg_pair():
        return remote(seg_all.at[me], seg_all.at[me], seg_send.at[0], seg_recv.at[0], partner)

    def seg_copy(slot, step):
        both = seg_all.at[pl.ds(pair0, 2)]
        return remote(both, both, seg_send.at[slot], seg_recv.at[slot], me + 2 * step)

    def seg_came(slot, step):
        both = seg_all.at[pl.ds(pair0 - 2 * step, 2)]
        remote(both, both, seg_send.at[slot], seg_recv.at[slot], partner).wait_recv()

    steps = [(1, 1), (2, -1), (3, 2), (4, -2), (5, 3), (6, -3)]

    def inside_row(step):
        return (chip + step >= 0) & (chip + step < chips)

    def seg_to(step):
        seg_copy(2 * abs(step) - 1 + (step < 0), step).start()

    def send_own(h):
        @pl.when(has_ahead)
        def _():
            own_ahead(h).start()

        @pl.when(col == 0)
        def _():
            own_across(h).start()

    local_seg.wait()
    seg_pair().start()
    tell(known.at[0], across)
    tell_planes(known.at[1], known.at[2])
    send_own(0)
    remote(
        seg_all.at[partner], seg_all.at[partner], seg_send.at[0], seg_recv.at[0], partner
    ).wait_recv()

    @pl.when(has_ahead)
    def _():
        seg_to(2)

    @pl.when(has_mid)
    def _():
        seg_to(-2)

    @pl.when(col == 0)
    def _():
        seg_to(1)

    @pl.when(col == 1)
    def _():
        seg_to(-1)

    pl.semaphore_wait(known.at[0], 1)
    tell_planes(known.at[3], known.at[4])

    @pl.when(has_ahead & (col == 0))
    def _():
        seg_to(3)

    @pl.when(has_ahead & (col == 1))
    def _():
        seg_to(1)

    @pl.when(has_mid)
    def _():
        pl.semaphore_wait(known.at[1], 1)

    @pl.when(has_mid & (col == 0))
    def _():
        seg_to(-1)

    @pl.when(has_mid & (col == 1))
    def _():
        seg_to(-3)

    send_own(1)

    @pl.when(has_ahead)
    def _():
        pl.semaphore_wait(known.at[2], 1)
        pl.semaphore_wait(known.at[4], 1)

    @pl.when(has_mid)
    def _():
        pl.semaphore_wait(known.at[3], 1)

    @pl.when((plane >= 2) & (col == 0))
    def _():
        seg_to(-3)

    @pl.when((plane < planes - 2) & (col == 1))
    def _():
        seg_to(3)

    for h in range(2, kv_count):
        send_own(h)

    @pl.when(core == 0)
    def _():
        for h in range(kv_count):
            own_pair(h).start()

    for small in smalls:
        small.wait()
    lane = lax.broadcasted_iota(jnp.int32, (tok, tok), 1)
    mine = jnp.broadcast_to(seg_all[me], (tok, tok)).astype(jnp.float32)
    mine = jnp.transpose(mine)
    belongs = jnp.where(mine == lane.astype(jnp.float32), 1.0, 0.0)
    lane8 = lax.broadcasted_iota(jnp.int32, (ratio, tok), 1)
    row8 = lax.broadcasted_iota(jnp.int32, (ratio, tok), 0)
    local_q.wait()
    for h in range(kv_count):
        q_s[h, :, :width] = q_raw[:, ratio * h:ratio * (h + 1), :].reshape(tok * ratio, width)
        gain = jnp.zeros((ratio, tok), jnp.float32)
        for r in range(ratio):
            gain = jnp.where(row8 == r, steer_ref[ratio * h + r].astype(jnp.float32), gain)
        gain = jnp.where((lane8 >= docs) & (lane8 < docs + len(parts)), gain, 0.0)
        more = belongs[:, None, :] + gain[None]
        q_s[h, :, width:] = more.reshape(tok * ratio, tok).astype(jnp.bfloat16)

    def take_mid(h):
        @pl.when(has_mid)
        def _():
            arrived_link(0, mid, core, h)

            @pl.when(col == 1)
            def _():
                mid_across(h).start()
            mid_pair(h).start()

    def take_near(h):
        @pl.when(has_near)
        def _():
            arrived_link(1, near, core, h)

            @pl.when(has_ahead)
            def _():
                near_ahead(h).start()
            near_pair(h).start()

    def take_rest(h):
        @pl.when(has_rest & (core == 1))
        def _():
            arrived_link(2, rest, core, h)
            rest_pair(h).start()

    take_mid(0)
    take_mid(1)
    take_mid(2)
    for slot, step in steps:
        @pl.when(inside_row(-step))
        def _():
            seg_came(slot, step)

    every = seg_all[:, 0, :]
    low, high = [], []
    row_low = jnp.zeros((ratio, tok), jnp.int32)
    row_high = jnp.zeros((ratio, tok), jnp.int32)
    before = 2 * tok * jnp.maximum(chip - 3, 0)
    for s in range(docs):
        many = jnp.sum((every == s).astype(jnp.int32))
        low.append(before + lax.rem(off_ref[s], jnp.maximum(many, 1)))
        row_low = jnp.where(row8 == s, before, row_low)
        before = before + many
        row_high = jnp.where(row8 == s, before, row_high)
        high.append(jnp.minimum(low[s] + width_ref[s], before))
    row_part = jnp.zeros((ratio, tok), jnp.float32)
    for n, part in enumerate(parts):
        row_part = jnp.where(row8 == docs + n, part, row_part)
    blocks = (
        me, pair0 - 4, pair0 - 3, pair0 - 2, pair0 - 1,
        jnp.where(core == 0, pair0 - 6, pair0), pair0 - 5,
    )
    padding = jnp.zeros((tok - ratio, tok), jnp.float32)
    for slot, block in enumerate(blocks):
        key_pos = block * tok + lane8
        inside = (key_pos >= low[0]) & (key_pos < high[0])
        for s in range(1, docs):
            inside = inside | ((key_pos >= low[s]) & (key_pos < high[s]))
        outside = (key_pos < row_low) | (key_pos >= row_high)
        seg_rows = jnp.where(outside, NEG_BIG, 0.0)
        part_rows = jnp.where(inside, 0.0, row_part)
        rows = jnp.where(row8 < docs, seg_rows, part_rows)
        rows = jnp.transpose(jnp.concatenate([rows, padding], axis=0))
        k_more[slot * tok:(slot + 1) * tok, :] = rows.astype(jnp.bfloat16)
    later = lane > lax.broadcasted_iota(jnp.int32, (tok, tok), 0)
    pen[...] = jnp.where(later, NEG_BIG, 0.0)

    factor = width ** (-0.5) * LOG2E
    tok_t = tok // TILES
    row_t = tok_t * ratio

    def visit(heads, refs_of, slot, first):
        refs_of = [refs_of(h) for h in heads]
        held_refs = len(refs_of[0])
        size = held_refs * tok
        extra = k_more[slot * tok:slot * tok + size, :]
        keys, values = [], []
        for refs in refs_of:
            key = jnp.concatenate([ref[0] for ref in refs], axis=0)
            keys.append(jnp.concatenate([key, extra], axis=1))
            value = jnp.concatenate([ref[1] for ref in refs], axis=0)
            values.append(jnp.concatenate([value, jnp.ones_like(value)], axis=1))

        def scores(n, i):
            return lax.dot_general(
                q_s[heads[n], i * row_t:(i + 1) * row_t, :], keys[n], (((1,), (1,)), ((), ())),
                preferred_element_type=jnp.float32,
            ).reshape(tok_t, ratio, size)

        todo = [(n, i) for n in range(len(heads)) for i in range(TILES)]
        following = scores(*todo[0])
        for at, (n, i) in enumerate(todo):
            h = heads[n]
            toks = slice(i * tok_t, (i + 1) * tok_t)
            raw = following
            if at + 1 < len(todo):
                following = scores(*todo[at + 1])
            pieces = [raw[:, :, k * tok:(k + 1) * tok] for k in range(held_refs)]
            if first:
                pieces[0] = pieces[0] + pen[toks, :][:, None, :]
            peak = pieces[0]
            for piece in pieces[1:]:
                peak = jnp.maximum(peak, piece)
            peak = jnp.max(peak, axis=2, keepdims=True)
            if first:
                top = jnp.broadcast_to(peak, (tok_t, ratio, tok))
                m_s[h, toks] = top
            else:
                held = m_s[h, toks]
                top = jnp.maximum(held, peak)
                shrink = jnp.exp2((held - top) * factor)
            packed = jnp.concatenate(
                [
                    jnp.exp2((piece - top) * factor).reshape(row_t, tok).astype(jnp.bfloat16)
                    for piece in pieces
                ],
                axis=1,
            )
            both = jnp.dot(packed, values[n], preferred_element_type=jnp.float32)
            both = both.reshape(tok_t, ratio, 2 * width)
            if first:
                acc[h, toks] = both
            else:
                weighted = both[:, :, :width] + acc[h, toks, :, :width] * shrink
                total = both[:, :, width:] + acc[h, toks, :, width:] * shrink
                out_ref[toks, ratio * h:ratio * (h + 1), :] = (weighted / total).astype(jnp.bfloat16)

    def visit_early(heads):
        @pl.when(has_mid)
        def _():
            for h in heads:
                arrived_pair(0, mid, 1 - core, h)
        visit(heads, lambda h: [own.at[h], mid.at[0, h], mid.at[1, h]], 0, True)

    def visit_late(heads):
        @pl.when(has_near)
        def _():
            for h in heads:
                arrived_pair(1, near, 1 - core, h)

        @pl.when(has_rest & (core == 0))
        def _():
            for h in heads:
                arrived_link(2, rest, core, h)

        @pl.when((core == 1) | has_rest)
        def _():
            for h in heads:
                arrived_pair(2, rest, 1 - core, h)
        visit(
            heads, lambda h: [near.at[0, h], near.at[1, h], rest.at[0, h], rest.at[1, h]], 3, False
        )

    take_mid(3)
    take_near(0)
    visit_early([0, 1])
    take_near(1)
    take_near(2)
    visit_early([2, 3])
    take_near(3)
    take_rest(0)
    take_rest(1)
    visit_late([0, 1])
    take_rest(2)
    visit_late([2])
    take_rest(3)
    visit_late([3])
    seg_pair().wait_send()
    for slot, step in steps:
        @pl.when(inside_row(step))
        def _():
            seg_copy(slot, step).wait_send()

    for h in range(kv_count):
        @pl.when(has_ahead)
        def _():
            own_ahead(h).wait_send()

        @pl.when(col == 0)
        def _():
            own_across(h).wait_send()

        @pl.when(core == 0)
        def _():
            own_pair(h).wait_send()

        @pl.when(has_mid)
        def _():
            mid_pair(h).wait_send()

        @pl.when(has_mid & (col == 1))
        def _():
            mid_across(h).wait_send()

        @pl.when(has_near)
        def _():
            near_pair(h).wait_send()

        @pl.when(has_near & has_ahead)
        def _():
            near_ahead(h).wait_send()

        @pl.when(has_rest & (core == 1))
        def _():
            rest_pair(h).wait_send()


def plane_device(query, keys, values, segment, instr_offset, instr_width, steer):
    tok, heads, width = query.shape
    kv_count = keys.shape[1]
    ratio = heads // kv_count
    count = lax.axis_size("ctx")
    keys, values = keys.reshape(tok * kv_count, width), values.reshape(tok * kv_count, width)
    hbm = pl.BlockSpec(memory_space=pltpu.HBM)
    pair = pltpu.VMEM((2, kv_count, 2, tok, width), jnp.bfloat16)
    dma = pltpu.SemaphoreType.DMA
    return pl.pallas_call(
        block_kernel,
        out_shape=jax.ShapeDtypeStruct(query.shape, query.dtype),
        in_specs=[hbm] * 7,
        out_specs=pl.BlockSpec(memory_space=pltpu.VMEM),
        scratch_shapes=[
            pltpu.VMEM(query.shape, jnp.bfloat16),
            pltpu.VMEM((kv_count, tok * ratio, 2 * width), jnp.bfloat16),
            pltpu.VMEM((2, tok * kv_count, width), jnp.bfloat16),
            pltpu.VMEM((2, tok * kv_count, width), jnp.float32),
            pltpu.VMEM((kv_count, 2, tok, width), jnp.bfloat16),
            pair, pair, pair,
            pltpu.VMEM((count, 1, tok), jnp.int32),
            pltpu.VMEM((tok, tok), jnp.float32),
            pltpu.VMEM((7 * tok, tok), jnp.bfloat16),
            pltpu.VMEM((kv_count, tok, ratio, width), jnp.float32),
            pltpu.VMEM((kv_count, tok, ratio, 2 * width), jnp.float32),
            pltpu.SMEM(steer.shape, jnp.int32),
            pltpu.SMEM(instr_offset.shape, jnp.int32),
            pltpu.SMEM(instr_width.shape, jnp.int32),
            dma((7,)), dma((7,)), dma((7,)),
            dma((3, kv_count)), dma((3, kv_count)), dma((3, kv_count)), dma((5, kv_count)),
            pltpu.SemaphoreType.REGULAR((5,)),
        ],
        compiler_params=pltpu.CompilerParams(
            collective_id=0, has_side_effects=True, vmem_limit_bytes=55000000
        ),
    )(*[pltpu.with_memory_space_constraint(x, pltpu.HBM) for x in (query, keys, values, segment.reshape(1, tok), steer, instr_offset, instr_width)])


def per_device(query, keys, values, segment, instr_offset, instr_width, steer):
    plan = plane_device if lax.axis_size("ctx") == 16 else ring_device
    return plan(query, keys, values, segment, instr_offset, instr_width, steer)


def solution(mesh):
    in_specs = (
        P(("groups", "ctx"), None, None),
        P(("groups", "ctx"), None, None),
        P(("groups", "ctx"), None, None),
        P(("groups", "ctx")),
        P("groups"),
        P("groups"),
        P(),
    )
    out_specs = P(("groups", "ctx"), None, None)
    return jax.shard_map(
        per_device, mesh=mesh, in_specs=in_specs, out_specs=out_specs, check_vma=False
    )
```

```python
import jax
import jax.numpy as jnp
import numpy as np
from jax import lax
from jax.experimental import pallas as pl
from jax.experimental.pallas import tpu as pltpu
from jax.sharding import PartitionSpec as P

NEG_BIG = -1e30
LOG_COEF = -4.605170185988091
LOG2E = 1.4426950408889634
TILES = 4
OVER = 2


def passed_along(value, axis, steps):
    count = lax.axis_size(axis)
    initial, last = (max(0, -steps), min(count, count - steps))
    return lax.ppermute(value, axis, [(source, source + steps) for source in range(initial, last)])


def prompt_tables(segment, instr_offset, instr_width):
    labels = jnp.arange(instr_offset.shape[0], dtype=jnp.int32)
    local_counts = jnp.sum((segment[:, None] == labels[None, :]).astype(jnp.int32), axis=0)
    counts = lax.psum(local_counts, "ctx")
    starts = jnp.cumsum(counts) - counts
    instr_lo = starts + instr_offset % counts
    instr_hi = jnp.minimum(instr_lo + instr_width, starts + counts)
    return (starts, instr_lo, instr_hi, labels)


def key_flags(key_pos, tables):
    starts, instr_lo, instr_hi, labels = tables
    key_seg = jnp.sum((starts[None, :] <= key_pos[:, None]).astype(jnp.int32), axis=1) - 1
    picked = key_seg[:, None] == labels[None, :]
    low_edge = jnp.sum(jnp.where(picked, instr_lo[None, :], 0), axis=1)
    high_edge = jnp.sum(jnp.where(picked, instr_hi[None, :], 0), axis=1)
    return (key_seg, (key_pos >= low_edge) & (key_pos < high_edge))


def update(carry_state, query_grouped_rows, key_value_block_length, allowed, inside, steer_gain):
    running, total, output_running_sum = carry_state
    logit_scores = jnp.einsum(
        "aecy,uey->ecau",
        query_grouped_rows,
        key_value_block_length[0],
        preferred_element_type=jnp.float32,
    )
    logit_scores = logit_scores * query_grouped_rows.shape[3] ** (-0.5)
    bias = steer_gain[:, :, None, None] * jnp.where(inside, 0.0, LOG_COEF)[None, None, None, :]
    logit_scores = jnp.where(allowed[None, None], logit_scores + bias, NEG_BIG)
    new_max = jnp.maximum(running, jnp.max(logit_scores, axis=3, keepdims=True))
    shrink = jnp.exp(running - new_max)
    probs = jnp.where(allowed[None, None], jnp.exp(logit_scores - new_max), 0.0)
    total = total * shrink + jnp.sum(probs, axis=3, keepdims=True)
    weighted = jnp.einsum(
        "cfqj,jcz->cfqz",
        probs.astype(jnp.bfloat16),
        key_value_block_length[1],
        preferred_element_type=jnp.float32,
    )
    return (new_max, total, output_running_sum * shrink + weighted)


def ring_device(query, keys, values, segment, instr_offset, instr_width, steer):
    tok_rows = query.shape[0]
    head_count = query.shape[1]
    head_width = query.shape[2]
    kv_count = keys.shape[1]
    ratio = head_count // kv_count
    reach_most = 3 * lax.axis_size("ctx") // 8
    query_grouped_rows = query.reshape(tok_rows, kv_count, ratio, head_width)
    position = lax.axis_index("ctx")
    offsets = jnp.arange(tok_rows, dtype=jnp.int32)
    query_pos = position * tok_rows + offsets
    tables = prompt_tables(segment, instr_offset, instr_width)
    steer_gain = steer.astype(jnp.float32).reshape(kv_count, ratio)
    stat_shape = (kv_count, ratio, tok_rows, 1)
    carry_state = (
        jnp.full(stat_shape, NEG_BIG, jnp.float32),
        jnp.zeros(stat_shape, jnp.float32),
        jnp.zeros((kv_count, ratio, tok_rows, head_width), jnp.float32),
    )

    def visit(held_state, key_value_block_length, hops_back):
        key_pos = (position - hops_back) * tok_rows + offsets
        key_seg, inside = key_flags(key_pos, tables)
        allowed = (key_seg[None, :] == segment[:, None]) & (key_pos[None, :] <= query_pos[:, None])
        return update(
            held_state, query_grouped_rows, key_value_block_length, allowed, inside, steer_gain
        )

    own_kv = jnp.stack([keys, values])
    carry_state = visit(carry_state, own_kv, 0)

    def loop_step(hop_count, loop_carry):
        held_state, current_kv = loop_carry
        current_kv = passed_along(current_kv, "ctx", 1)
        return (visit(held_state, current_kv, hop_count), current_kv)

    carry_state, _ = lax.fori_loop(1, reach_most + 1, loop_step, (carry_state, own_kv))
    running, total, output_running_sum = carry_state
    result = (output_running_sum / total).astype(jnp.bfloat16)
    return result.transpose(2, 0, 1, 3).reshape(tok_rows, head_count, head_width)


def bias_parts(width):
    left, parts = LOG_COEF * width ** 0.5, []
    for _ in range(3):
        parts.append(float(np.float32(left).astype(jnp.bfloat16)))
        left = left - parts[-1]
    return parts


def block_kernel(
    q_hbm, k_hbm, v_hbm, seg_hbm, steer_hbm, off_hbm, width_hbm,
    out_ref,
    q_raw, q_s, kv_raw, kv_wide, own, near, mid, rest, seg_all, pen, k_more, m_s, acc,
    steer_ref, off_ref, width_ref,
    in_sem, seg_send, seg_recv, link_recv, pair_recv, own_send, fwd_send, known,
):
    count = lax.axis_size("ctx")
    kv_count, tok = own.shape[0], own.shape[2]
    width = own.shape[3]
    ratio = q_raw.shape[1] // kv_count
    docs = off_ref.shape[0]
    parts = bias_parts(width)
    me = lax.axis_index("ctx")
    core = lax.rem(me, 2)
    chip = me // 2
    col = lax.rem(chip, 2)
    plane = chip // 2
    partner = me + 1 - 2 * core
    across = me + 2 - 4 * col
    ahead = me + 4
    behind = me - 4
    planes = count // 4
    chips = count // 2
    pair0 = 2 * chip

    def remote(src, dst, send, recv, target):
        return pltpu.make_async_remote_copy(
            src_ref=src, dst_ref=dst, send_sem=send, recv_sem=recv,
            device_id={"ctx": target}, device_id_type=pl.DeviceIdType.MESH,
        )

    has_ahead = ahead < count
    has_mid = plane >= 1
    has_near = chip >= 1
    has_rest = chip >= 3
    beside = jnp.minimum(plane, 1) + jnp.minimum(planes - 1 - plane, 1)

    def tell(sem, target):
        pl.semaphore_signal(
            sem, inc=1, device_id={"ctx": target}, device_id_type=pl.DeviceIdType.MESH
        )

    def tell_planes(to_ahead, to_behind):
        @pl.when(has_ahead)
        def _():
            tell(to_ahead, ahead)

        @pl.when(has_mid)
        def _():
            tell(to_behind, behind)

    local_k = pltpu.make_async_copy(k_hbm, kv_raw.at[0], in_sem.at[1])
    local_v = pltpu.make_async_copy(v_hbm, kv_raw.at[1], in_sem.at[3])
    local_seg = pltpu.make_async_copy(seg_hbm, seg_all.at[me], in_sem.at[2])
    local_q = pltpu.make_async_copy(q_hbm, q_raw, in_sem.at[0])
    smalls = [
        pltpu.make_async_copy(src, dst, in_sem.at[4 + n])
        for n, (src, dst) in enumerate(
            ((steer_hbm, steer_ref), (off_hbm, off_ref), (width_hbm, width_ref))
        )
    ]
    local_k.start()
    local_v.start()
    seg_all[...] = jnp.full(seg_all.shape, -1, jnp.int32)
    barrier = pltpu.get_barrier_semaphore()
    tell(barrier, partner)
    tell(barrier, across)
    tell_planes(barrier, barrier)
    local_seg.start()
    local_q.start()
    for small in smalls:
        small.start()

    @pl.when(jnp.logical_not(has_mid))
    def _():
        mid[...] = jnp.zeros_like(mid)

    @pl.when(jnp.logical_not(has_near))
    def _():
        near[...] = jnp.zeros_like(near)

    @pl.when(jnp.logical_not(has_rest))
    def _():
        rest[1] = jnp.zeros_like(rest[1])

    @pl.when(jnp.logical_not(has_rest) & (core == 0))
    def _():
        rest[0] = jnp.zeros_like(rest[0])

    for n, local in enumerate((local_k, local_v)):
        local.wait()
        kv_wide[n] = kv_raw[n].astype(jnp.float32)
        for h in range(kv_count):
            rows = kv_wide[n, pl.ds(h, tok, stride=kv_count), :]
            own[h, n] = rows.astype(jnp.bfloat16)

    pl.semaphore_wait(barrier, 2 + beside)

    def own_ahead(h):
        return remote(own.at[h], mid.at[core, h], own_send.at[0, h], link_recv.at[0, h], ahead)

    def own_across(h):
        return remote(own.at[h], near.at[core, h], own_send.at[1, h], link_recv.at[1, h], across)

    def own_pair(h):
        return remote(own.at[h], rest.at[0, h], own_send.at[2, h], pair_recv.at[2, h], partner)

    def mid_pair(h):
        return remote(mid.at[core, h], mid.at[core, h], fwd_send.at[0, h], pair_recv.at[0, h], partner)

    def mid_across(h):
        return remote(mid.at[core, h], near.at[core, h], fwd_send.at[1, h], link_recv.at[1, h], across)

    def mid_over(h):
        return remote(mid.at[core, h], rest.at[core, h], fwd_send.at[5, h], link_recv.at[2, h], across)

    def goes_over(h):
        return h >= kv_count - OVER

    def near_pair(h):
        return remote(near.at[core, h], near.at[core, h], fwd_send.at[2, h], pair_recv.at[1, h], partner)

    def near_ahead(h):
        return remote(near.at[core, h], rest.at[core, h], fwd_send.at[3, h], link_recv.at[2, h], ahead)

    def rest_pair(h):
        return remote(rest.at[1, h], rest.at[1, h], fwd_send.at[4, h], pair_recv.at[2, h], partner)

    def arrived_link(kind, buf, slot, h):
        remote(buf.at[slot, h], buf.at[slot, h], own_send.at[0, h], link_recv.at[kind, h], partner).wait_recv()

    def arrived_pair(kind, buf, slot, h):
        remote(buf.at[slot, h], buf.at[slot, h], own_send.at[0, h], pair_recv.at[kind, h], partner).wait_recv()

    def seg_pair():
        return remote(seg_all.at[me], seg_all.at[me], seg_send.at[0], seg_recv.at[0], partner)

    def seg_copy(slot, step):
        both = seg_all.at[pl.ds(pair0, 2)]
        return remote(both, both, seg_send.at[slot], seg_recv.at[slot], me + 2 * step)

    def seg_came(slot, step):
        both = seg_all.at[pl.ds(pair0 - 2 * step, 2)]
        remote(both, both, seg_send.at[slot], seg_recv.at[slot], partner).wait_recv()

    steps = [(1, 1), (2, -1), (3, 2), (4, -2), (5, 3), (6, -3)]

    def inside_row(step):
        return (chip + step >= 0) & (chip + step < chips)

    def seg_to(step):
        seg_copy(2 * abs(step) - 1 + (step < 0), step).start()

    def send_own(h):
        @pl.when(has_ahead)
        def _():
            own_ahead(h).start()

        @pl.when(col == 0)
        def _():
            own_across(h).start()

    local_seg.wait()
    seg_pair().start()
    tell(known.at[0], across)
    tell_planes(known.at[1], known.at[2])
    send_own(0)
    remote(
        seg_all.at[partner], seg_all.at[partner], seg_send.at[0], seg_recv.at[0], partner
    ).wait_recv()

    @pl.when(has_ahead)
    def _():
        seg_to(2)

    @pl.when(has_mid)
    def _():
        seg_to(-2)

    @pl.when(col == 0)
    def _():
        seg_to(1)

    @pl.when(col == 1)
    def _():
        seg_to(-1)

    pl.semaphore_wait(known.at[0], 1)
    tell_planes(known.at[3], known.at[4])

    @pl.when(has_ahead & (col == 0))
    def _():
        seg_to(3)

    @pl.when(has_ahead & (col == 1))
    def _():
        seg_to(1)

    @pl.when(has_mid)
    def _():
        pl.semaphore_wait(known.at[1], 1)

    @pl.when(has_mid & (col == 0))
    def _():
        seg_to(-1)

    @pl.when(has_mid & (col == 1))
    def _():
        seg_to(-3)

    send_own(1)

    @pl.when(has_ahead)
    def _():
        pl.semaphore_wait(known.at[2], 1)
        pl.semaphore_wait(known.at[4], 1)

    @pl.when(has_mid)
    def _():
        pl.semaphore_wait(known.at[3], 1)

    @pl.when((plane >= 2) & (col == 0))
    def _():
        seg_to(-3)

    @pl.when((plane < planes - 2) & (col == 1))
    def _():
        seg_to(3)

    for h in range(2, kv_count):
        send_own(h)

    @pl.when(core == 0)
    def _():
        for h in range(kv_count):
            own_pair(h).start()

    for small in smalls:
        small.wait()
    lane = lax.broadcasted_iota(jnp.int32, (tok, tok), 1)
    mine = jnp.broadcast_to(seg_all[me], (tok, tok)).astype(jnp.float32)
    mine = jnp.transpose(mine)
    belongs = jnp.where(mine == lane.astype(jnp.float32), 1.0, 0.0)
    lane8 = lax.broadcasted_iota(jnp.int32, (ratio, tok), 1)
    row8 = lax.broadcasted_iota(jnp.int32, (ratio, tok), 0)
    local_q.wait()
    for h in range(kv_count):
        q_s[h, :, :width] = q_raw[:, ratio * h:ratio * (h + 1), :].reshape(tok * ratio, width)
        gain = jnp.zeros((ratio, tok), jnp.float32)
        for r in range(ratio):
            gain = jnp.where(row8 == r, steer_ref[ratio * h + r].astype(jnp.float32), gain)
        gain = jnp.where((lane8 >= docs) & (lane8 < docs + len(parts)), gain, 0.0)
        more = belongs[:, None, :] + gain[None]
        q_s[h, :, width:] = more.reshape(tok * ratio, tok).astype(jnp.bfloat16)

    def take_mid(h):
        @pl.when(has_mid)
        def _():
            arrived_link(0, mid, core, h)

            @pl.when(col == 1)
            def _():
                mid_across(h).start()

            if goes_over(h):
                @pl.when(col == 0)
                def _():
                    mid_over(h).start()
            mid_pair(h).start()

    def take_near(h):
        @pl.when(has_near)
        def _():
            arrived_link(1, near, core, h)

            @pl.when((has_ahead & (col == 0)) if goes_over(h) else has_ahead)
            def _():
                near_ahead(h).start()
            near_pair(h).start()

    def take_rest(h):
        @pl.when(has_rest & (core == 1))
        def _():
            arrived_link(2, rest, core, h)
            rest_pair(h).start()

    take_mid(0)
    take_mid(1)
    take_mid(2)
    take_mid(3)
    take_near(0)
    for slot, step in steps:
        @pl.when(inside_row(-step))
        def _():
            seg_came(slot, step)

    every = seg_all[:, 0, :]
    low, high = [], []
    row_low = jnp.zeros((ratio, tok), jnp.int32)
    row_high = jnp.zeros((ratio, tok), jnp.int32)
    before = 2 * tok * jnp.maximum(chip - 3, 0)
    for s in range(docs):
        many = jnp.sum((every == s).astype(jnp.int32))
        low.append(before + lax.rem(off_ref[s], jnp.maximum(many, 1)))
        row_low = jnp.where(row8 == s, before, row_low)
        before = before + many
        row_high = jnp.where(row8 == s, before, row_high)
        high.append(jnp.minimum(low[s] + width_ref[s], before))
    row_part = jnp.zeros((ratio, tok), jnp.float32)
    for n, part in enumerate(parts):
        row_part = jnp.where(row8 == docs + n, part, row_part)
    blocks = (
        me, pair0 - 4, pair0 - 3, pair0 - 2, pair0 - 1,
        jnp.where(core == 0, pair0 - 6, pair0), pair0 - 5,
    )
    padding = jnp.zeros((tok - ratio, tok), jnp.float32)
    for slot, block in enumerate(blocks):
        key_pos = block * tok + lane8
        inside = (key_pos >= low[0]) & (key_pos < high[0])
        for s in range(1, docs):
            inside = inside | ((key_pos >= low[s]) & (key_pos < high[s]))
        outside = (key_pos < row_low) | (key_pos >= row_high)
        seg_rows = jnp.where(outside, NEG_BIG, 0.0)
        part_rows = jnp.where(inside, 0.0, row_part)
        rows = jnp.where(row8 < docs, seg_rows, part_rows)
        rows = jnp.transpose(jnp.concatenate([rows, padding], axis=0))
        k_more[slot * tok:(slot + 1) * tok, :] = rows.astype(jnp.bfloat16)
    later = lane > lax.broadcasted_iota(jnp.int32, (tok, tok), 0)
    pen[...] = jnp.where(later, NEG_BIG, 0.0)

    factor = width ** (-0.5) * LOG2E
    tok_t = tok // TILES
    row_t = tok_t * ratio

    def visit(heads, refs_of, slot, first):
        refs_of = [refs_of(h) for h in heads]
        held_refs = len(refs_of[0])
        size = held_refs * tok
        extra = k_more[slot * tok:slot * tok + size, :]
        keys, values = [], []
        for refs in refs_of:
            key = jnp.concatenate([ref[0] for ref in refs], axis=0)
            keys.append(jnp.concatenate([key, extra], axis=1))
            value = jnp.concatenate([ref[1] for ref in refs], axis=0)
            values.append(jnp.concatenate([value, jnp.ones_like(value)], axis=1))

        def scores(n, i):
            return lax.dot_general(
                q_s[heads[n], i * row_t:(i + 1) * row_t, :], keys[n], (((1,), (1,)), ((), ())),
                preferred_element_type=jnp.float32,
            ).reshape(tok_t, ratio, size)

        todo = [(n, i) for n in range(len(heads)) for i in range(TILES)]
        following = scores(*todo[0])
        for at, (n, i) in enumerate(todo):
            h = heads[n]
            toks = slice(i * tok_t, (i + 1) * tok_t)
            raw = following
            if at + 1 < len(todo):
                following = scores(*todo[at + 1])
            pieces = [raw[:, :, k * tok:(k + 1) * tok] for k in range(held_refs)]
            if first:
                pieces[0] = pieces[0] + pen[toks, :][:, None, :]
            peak = pieces[0]
            for piece in pieces[1:]:
                peak = jnp.maximum(peak, piece)
            peak = jnp.max(peak, axis=2, keepdims=True)
            if first:
                top = jnp.broadcast_to(peak, (tok_t, ratio, tok))
                m_s[h, toks] = top
            else:
                held = m_s[h, toks]
                top = jnp.maximum(held, peak)
                shrink = jnp.exp2((held - top) * factor)
            packed = jnp.concatenate(
                [
                    jnp.exp2((piece - top) * factor).reshape(row_t, tok).astype(jnp.bfloat16)
                    for piece in pieces
                ],
                axis=1,
            )
            both = jnp.dot(packed, values[n], preferred_element_type=jnp.float32)
            both = both.reshape(tok_t, ratio, 2 * width)
            if first:
                acc[h, toks] = both
            else:
                weighted = both[:, :, :width] + acc[h, toks, :, :width] * shrink
                total = both[:, :, width:] + acc[h, toks, :, width:] * shrink
                out_ref[toks, ratio * h:ratio * (h + 1), :] = (weighted / total).astype(jnp.bfloat16)

    def visit_early(heads):
        @pl.when(has_mid)
        def _():
            for h in heads:
                arrived_pair(0, mid, 1 - core, h)
        visit(heads, lambda h: [own.at[h], mid.at[0, h], mid.at[1, h]], 0, True)

    def visit_late(heads):
        @pl.when(has_near)
        def _():
            for h in heads:
                arrived_pair(1, near, 1 - core, h)

        @pl.when(has_rest & (core == 0))
        def _():
            for h in heads:
                arrived_link(2, rest, core, h)

        @pl.when((core == 1) | has_rest)
        def _():
            for h in heads:
                arrived_pair(2, rest, 1 - core, h)
        visit(
            heads, lambda h: [near.at[0, h], near.at[1, h], rest.at[0, h], rest.at[1, h]], 3, False
        )

    take_near(1)
    visit_early([0, 1])
    take_near(2)
    visit_early([2, 3])
    take_near(3)
    take_rest(0)
    take_rest(1)
    visit_late([0, 1])
    take_rest(2)
    visit_late([2])
    take_rest(3)
    visit_late([3])
    seg_pair().wait_send()
    for slot, step in steps:
        @pl.when(inside_row(step))
        def _():
            seg_copy(slot, step).wait_send()

    for h in range(kv_count):
        @pl.when(has_ahead)
        def _():
            own_ahead(h).wait_send()

        @pl.when(col == 0)
        def _():
            own_across(h).wait_send()

        @pl.when(core == 0)
        def _():
            own_pair(h).wait_send()

        @pl.when(has_mid)
        def _():
            mid_pair(h).wait_send()

        @pl.when(has_mid & (col == 1))
        def _():
            mid_across(h).wait_send()

        @pl.when(has_near)
        def _():
            near_pair(h).wait_send()

        @pl.when((has_near & has_ahead & (col == 0)) if goes_over(h) else (has_near & has_ahead))
        def _():
            near_ahead(h).wait_send()

        if goes_over(h):
            @pl.when(has_mid & (col == 0))
            def _():
                mid_over(h).wait_send()

        @pl.when(has_rest & (core == 1))
        def _():
            rest_pair(h).wait_send()


def plane_device(query, keys, values, segment, instr_offset, instr_width, steer):
    tok, heads, width = query.shape
    kv_count = keys.shape[1]
    ratio = heads // kv_count
    count = lax.axis_size("ctx")
    keys, values = keys.reshape(tok * kv_count, width), values.reshape(tok * kv_count, width)
    hbm = pl.BlockSpec(memory_space=pltpu.HBM)
    pair = pltpu.VMEM((2, kv_count, 2, tok, width), jnp.bfloat16)
    dma = pltpu.SemaphoreType.DMA
    return pl.pallas_call(
        block_kernel,
        out_shape=jax.ShapeDtypeStruct(query.shape, query.dtype),
        in_specs=[hbm] * 7,
        out_specs=pl.BlockSpec(memory_space=pltpu.VMEM),
        scratch_shapes=[
            pltpu.VMEM(query.shape, jnp.bfloat16),
            pltpu.VMEM((kv_count, tok * ratio, 2 * width), jnp.bfloat16),
            pltpu.VMEM((2, tok * kv_count, width), jnp.bfloat16),
            pltpu.VMEM((2, tok * kv_count, width), jnp.float32),
            pltpu.VMEM((kv_count, 2, tok, width), jnp.bfloat16),
            pair, pair, pair,
            pltpu.VMEM((count, 1, tok), jnp.int32),
            pltpu.VMEM((tok, tok), jnp.float32),
            pltpu.VMEM((7 * tok, tok), jnp.bfloat16),
            pltpu.VMEM((kv_count, tok, ratio, width), jnp.float32),
            pltpu.VMEM((kv_count, tok, ratio, 2 * width), jnp.float32),
            pltpu.SMEM(steer.shape, jnp.int32),
            pltpu.SMEM(instr_offset.shape, jnp.int32),
            pltpu.SMEM(instr_width.shape, jnp.int32),
            dma((7,)), dma((7,)), dma((7,)),
            dma((3, kv_count)), dma((3, kv_count)), dma((3, kv_count)), dma((6, kv_count)),
            pltpu.SemaphoreType.REGULAR((5,)),
        ],
        compiler_params=pltpu.CompilerParams(
            collective_id=0, has_side_effects=True, vmem_limit_bytes=55000000
        ),
    )(*[pltpu.with_memory_space_constraint(x, pltpu.HBM) for x in (query, keys, values, segment.reshape(1, tok), steer, instr_offset, instr_width)])


def per_device(query, keys, values, segment, instr_offset, instr_width, steer):
    plan = plane_device if lax.axis_size("ctx") == 16 else ring_device
    return plan(query, keys, values, segment, instr_offset, instr_width, steer)


def solution(mesh):
    in_specs = (
        P(("groups", "ctx"), None, None),
        P(("groups", "ctx"), None, None),
        P(("groups", "ctx"), None, None),
        P(("groups", "ctx")),
        P("groups"),
        P("groups"),
        P(),
    )
    out_specs = P(("groups", "ctx"), None, None)
    return jax.shard_map(
        per_device, mesh=mesh, in_specs=in_specs, out_specs=out_specs, check_vma=False
    )
```
